512 devices in a mesh: row: 8 (over z), col: 8 (over x, y_hi), pair: 8 (over y_lo, core).
Axes of the slice: x: 4, y: 8 (y_hi: 2, y_lo: 4; y = y_hi * 4 + y_lo), z: 8, core: 2. Of those that a mesh axis runs over, the one named last changes fastest.
Arguments:
- pair_slab: bfloat16 [3072, 16384], P('pair', 'row'), may hold values from -0.4375 to 0.4375
- pair_weights: float32 [3072], P('pair'), may hold values from 0.2 to 2
Outputs:
- polarizability: float32 [16384, 16384], P('row', ('col', 'pair'))
The draws below stay inside these ranges and needn't reach their ends.
All inputs are finite; a program needn't handle non-finite values.
Results may differ from the reference program's by a relative error of at most 0.0085.
Values may be sent and summed in bfloat16 or wider, within the bound.
A program may use at most 64 MiB of HBM per device.

```python
import math
import jax
import jax.numpy as jnp
from jax import lax

NAUX = 16384
NPAIR = 3072


def shard_levels(stream_key, shape, cuts, low, high):
    loudness, own = 1.0, jax.random.fold_in(stream_key, 6)
    for position, blocks in cuts:
        steps = jnp.exp(jax.random.uniform(jax.random.fold_in(own, position), (blocks,), jnp.float32, low / len(cuts), high / len(cuts)))
        loudness = loudness * jnp.repeat(steps, shape[position] // blocks).reshape([-1 if axis == position else 1 for axis in range(len(shape))])
    return loudness


def normal_values(stream_key, shape, deviation, bound, cuts=(), kind=jnp.bfloat16):
    factor_of = shard_levels(stream_key, shape, cuts, -0.22, 0.18) if cuts else 1.0
    result = jax.random.normal(stream_key, shape, jnp.float32) * deviation * factor_of
    return jnp.minimum(jnp.maximum(result, -bound), bound).astype(kind)


def setup_inputs(seed: int = 0) -> dict:
    key_of = jax.random.split(jax.random.key(seed), 3)
    pair_slab = normal_values(key_of[0], (NPAIR, NAUX), (NPAIR // 16) ** -0.5, 0.4375, ((0, 8), (1, 8)))
    pair_weights = jnp.clip(jnp.exp(math.log(2.0) - 2.3025851 * jax.random.uniform(key_of[1], (NPAIR,), jnp.float32) ** shard_levels(key_of[1], (NPAIR,), ((0, 8),), -0.2, 0.2)), 0.2, 2.0)
    return {"pair_slab": pair_slab, "pair_weights": pair_weights}


def reference(pair_slab, pair_weights):
    weighted = (pair_weights[:, None] * pair_slab.astype(jnp.float32)).astype(jnp.bfloat16)
    return lax.dot_general(weighted.astype(jnp.float32), pair_slab.astype(jnp.float32), (((0,), (0,)), ((), ())), precision=lax.Precision.HIGHEST, preferred_element_type=jnp.float32)
```

```python
import functools
import jax
import jax.numpy as jnp
from jax import lax
from jax.experimental import pallas as pl
from jax.experimental.pallas import tpu as pltpu
from jax.sharding import PartitionSpec as P

MESH = pl.DeviceIdType.MESH
NX, NY, NZ, NYL = 4, 8, 8, 4
DEPTH, ROWS, COLS = 384, 2048, 256
QUARTER, UNIT = ROWS // 4, DEPTH // 4

SLOTS = (
    (0, 1, 1), (0, 2, 1), (0, 1, 0), (1, 1, 1), (0, 3, 1), (0, 2, 0),
    (0, 0, 1), (1, 2, 1), (0, 3, 0), (1, 3, 1), (0, 0, 0), (1, 0, 1),
)
N = len(SLOTS)
START = (0, 1, 2)
AFTER = {1: (3, 4, 5, 6), 4: (7, 8), 6: (9, 10, 11)}
LAST = 13
CHUNKS = 16
PIECES = {
    7: ((0, 0), (0, 1)),
    8: ((0, 2), (0, 3)),
    11: ((-1, 0), (1, 0)),
    12: ((-1, 1), (1, -1), (-1, 2), (1, -2), (-1, 3), (1, -3)),
    13: ((2, 0), (2, 2), (2, 1), (2, 3)),
}
READY = {7: 0, 11: 1, 13: 2}


def mod(value, n):
    return lax.rem(value + 4 * n, n)


def kernel(slab, weight, out, panel, cols, scaled, wbuf, local, ysend, yrecv, xsend, xrecv, osend, orecv,
           sysend, syrecv, sxsend, sxrecv, zsend, zrecv, wsend, wrecv):
    z, col, pair = lax.axis_index("row"), lax.axis_index("col"), lax.axis_index("pair")
    x, yh, yl, c = col // 2, lax.rem(col, 2), pair // 2, lax.rem(pair, 2)
    y = yh * NYL + yl
    half = lax.rem(x, 2)

    def device(xx, yy, zz, cc):
        xx, yy, zz = mod(xx, NX), mod(yy, NY), mod(zz, NZ)
        return (zz, xx * 2 + yy // NYL, lax.rem(yy, NYL) * 2 + cc)

    ys = (device(x, y + 1, z, c), device(x, y - 1, z, c))
    xs = (device(x + 1, y, z, c), device(x - 1, y, z, c))
    zs = (device(x, y, z + 1, c), device(x, y, z - 1, c))
    sibling = device(x, y, z, 1 - c)

    def block(rel, flip):
        core = c + flip - 2 * c * flip
        return mod(yl + rel, NYL) * 2 + core

    def rows_at(rel, flip, group):
        return pl.ds(pl.multiple_of(block(rel, flip) * DEPTH + group * UNIT, 32), UNIT)

    def quarter_at(rel):
        return pl.ds(pl.multiple_of(mod(yl + rel, 4) * QUARTER, QUARTER), QUARTER)

    def unit(rel, flip, q, group):
        return panel.at[rows_at(rel, flip, group), quarter_at(q)]

    def remote(src, dst, send, recv, to):
        return pltpu.make_async_remote_copy(
            src_ref=src, dst_ref=dst, send_sem=send, recv_sem=recv, device_id=to, device_id_type=MESH
        )

    def group_of(d, low, own_half=True):
        return 2 * (half if own_half else 1 - half) + (low if d == 0 else 1 - low)

    def y_out(d, t):
        sign = 1 - 2 * d
        kind, q, low = SLOTS[t]
        piece = unit(-sign * kind, 0, sign * q, group_of(d, low))
        return remote(piece, piece, ysend.at[d, t], yrecv.at[d, t], ys[d])

    def arrived(d, t, own_half=True, flip=0):
        sign = 1 - 2 * d
        kind, q, low = SLOTS[t]
        return unit(-sign * (1 + kind), flip, sign * (q - 1), group_of(d, low, own_half))

    def y_in(d, t):
        piece = arrived(d, t)
        return remote(piece, piece, ysend.at[d, t], yrecv.at[d, t], ys[1 - d])

    def side(e, t):
        low = SLOTS[t][2]
        return 0 if low == e else 1

    def x_out(e, t):
        piece = arrived(side(e, t), t)
        return remote(piece, piece, xsend.at[e, t], xrecv.at[e, t], xs[e])

    def x_in(e, t):
        piece = arrived(side(e, t), t, own_half=False)
        return remote(piece, piece, xsend.at[e, t], xrecv.at[e, t], xs[1 - e])

    def sy(d, t, flip):
        piece = arrived(d, t, flip=flip)
        return remote(piece, piece, sysend.at[d, t], syrecv.at[d, t], sibling)

    def sx(e, t, flip):
        piece = arrived(side(e, t), t, own_half=False, flip=flip)
        return remote(piece, piece, sxsend.at[e, t], sxrecv.at[e, t], sibling)

    def own(q, flip):
        piece = panel.at[pl.ds(pl.multiple_of(block(0, flip) * DEPTH, DEPTH), DEPTH), quarter_at(q)]
        return remote(piece, piece, osend.at[q], orecv.at[q], sibling)

    def weights(n, rel, flip, to):
        piece = wbuf.at[block(rel, flip)]
        return remote(piece, piece, wsend.at[n], wrecv.at[n], to)

    column = pl.ds(pl.multiple_of(pair * COLS, COLS), COLS)
    distance = (mod(z - col, NZ), mod(col - z, NZ))

    def chunk(d, j, i):
        m = j // 2
        later = (m + 2) // 3
        sign = 1 - 2 * d
        rel = sign * (m + m // 2 - 2 * (m // 3))
        flip = (1 - later) * lax.rem(j, 2) + later * i
        part = (1 - later) * i + later * lax.rem(half + j, 2)
        return rows_at(rel, flip, 2 * part + d)

    def z_step(t, i):
        for d in range(2):
            j = t + 1 - distance[d]

            @pl.when((j >= 0) & (j < CHUNKS // 2))
            def _(d=d, j=j):
                rows = chunk(d, j, i)
                k = 2 * j + i

                @pl.when(distance[d] == 0)
                def _():
                    remote(panel.at[rows, column], cols.at[rows], zsend.at[d, k], zrecv.at[d, k], zs[d]).start()

                @pl.when(distance[d] > 0)
                def _():
                    remote(cols.at[rows], cols.at[rows], zsend.at[d, k], zrecv.at[d, k], zs[1 - d]).wait_recv()

                    @pl.when(distance[d] < NZ - 1)
                    def _():
                        remote(cols.at[rows], cols.at[rows], zsend.at[d, k], zrecv.at[d, k], zs[d]).start()

    def scale(rel):
        first = mod(yl + rel, NYL) * 2
        for b in range(2):
            for i in range(DEPTH // 128):
                at = pl.multiple_of((first + b) * DEPTH + i * 128, 128)
                w = wbuf[first + b, pl.ds(i, 1), :]

                @pl.when(z == col)
                def _(at=at, w=w):
                    tile = panel[pl.ds(at, 128), column].astype(jnp.float32)
                    scaled[:, pl.ds(at, 128)] = (jnp.transpose(tile) * w).astype(jnp.bfloat16)

                @pl.when(z != col)
                def _(at=at, w=w):
                    tile = cols[pl.ds(at, 128), :].astype(jnp.float32)
                    scaled[:, pl.ds(at, 128)] = (jnp.transpose(tile) * w).astype(jnp.bfloat16)

    def multiply(rel, q):
        at = pl.ds(pl.multiple_of(mod(yl + rel, NYL) * 2 * DEPTH, 2 * DEPTH), 2 * DEPTH)
        where = quarter_at(q)
        value = jnp.dot(scaled[:, at], panel[at, where], preferred_element_type=jnp.float32)
        if rel == 0:
            out[:, where] = value
        else:
            out[:, where] += value

    mine = pltpu.make_async_copy(slab, panel.at[pl.ds(pl.multiple_of(pair * DEPTH, DEPTH), DEPTH)], local.at[0])
    mine.start()
    my_weights = pltpu.make_async_copy(weight, wbuf.at[pair], local.at[1])
    my_weights.start()
    barrier = pltpu.get_barrier_semaphore()
    partners = ys + xs + zs + (sibling,)
    for to in partners:
        pl.semaphore_signal(barrier, inc=1, device_id=to, device_id_type=MESH)
    mine.wait()
    my_weights.wait()
    pl.semaphore_wait(barrier, len(partners))

    for t in START:
        for d in range(2):
            y_out(d, t).start()
    own(0, 0).start()
    z_step(-1, 0)
    z_step(-1, 1)
    for q in range(1, 4):
        own(q, 0).start()
    weights(0, 0, 0, ys[0]).start()
    weights(1, 0, 0, ys[1]).start()
    weights(2, 0, 0, sibling).start()

    for t in range(LAST + 1):
        if t < N:
            for d in range(2):
                y_in(d, t).wait_recv()
            for s in AFTER.get(t, ())[:1]:
                for d in range(2):
                    y_out(d, s).start()
            for e in range(2):
                x_out(e, t).start()
            for s in AFTER.get(t, ())[1:]:
                for d in range(2):
                    y_out(d, s).start()
            for d in range(2):
                sy(d, t, 0).start()
        if t == 0:
            own(0, 1).wait_recv()
        if 1 <= t <= N:
            for d in range(2):
                sy(d, t - 1, 1).wait_recv()
        z_step(t, 0)
        if 1 <= t <= N:
            for e in range(2):
                x_in(e, t - 1).wait_recv()
                sx(e, t - 1, 0).start()
        if 2 <= t <= N + 1:
            for e in range(2):
                sx(e, t - 2, 1).wait_recv()
        z_step(t, 1)
        if t == 1:
            weights(0, -1, 0, ys[1]).wait_recv()
            weights(1, 1, 0, ys[0]).wait_recv()
            weights(2, 0, 1, sibling).wait_recv()
            weights(3, -1, 0, ys[0]).start()
            weights(4, -1, 0, sibling).start()
            weights(5, 1, 0, sibling).start()
        if t == 2:
            for q in range(1, 4):
                own(q, 1).wait_recv()
        if t == 4:
            weights(3, 2, 0, ys[1]).wait_recv()
            weights(6, 2, 0, sibling).start()
            weights(4, -1, 1, sibling).wait_recv()
            weights(5, 1, 1, sibling).wait_recv()
        if t == 6:
            weights(6, 2, 1, sibling).wait_recv()
        if t in READY:
            for rel in {0: (0,), 1: (-1, 1), 2: (2,)}[READY[t]]:
                scale(rel)
        for rel, q in PIECES.get(t, ()):
            multiply(rel, q)

    for t in range(N):
        for d in range(2):
            y_out(d, t).wait_send()
            x_out(d, t).wait_send()
            sy(d, t, 0).wait_send()
            sx(d, t, 0).wait_send()
    for q in range(4):
        own(q, 0).wait_send()
    for n, (rel, to) in enumerate(((0, ys[0]), (0, ys[1]), (0, sibling), (-1, ys[0]), (-1, sibling), (1, sibling), (2, sibling))):
        weights(n, rel, 0, to).wait_send()
    for d in range(2):

        @pl.when(distance[d] < NZ - 1)
        def _(d=d):
            for k in range(CHUNKS):
                rows = pl.ds(k * UNIT, UNIT)
                remote(cols.at[rows], cols.at[rows], zsend.at[d, k], zrecv.at[d, k], zs[d]).wait_send()


def gather_and_multiply(slab, weight):
    dma = pltpu.SemaphoreType.DMA
    return pl.pallas_call(
        kernel,
        out_shape=jax.ShapeDtypeStruct((COLS, ROWS), jnp.float32),
        in_specs=[pl.BlockSpec(memory_space=pl.ANY)] * 2,
        out_specs=pl.BlockSpec(memory_space=pltpu.VMEM),
        scratch_shapes=[
            pltpu.VMEM((8 * DEPTH, ROWS), jnp.bfloat16),
            pltpu.VMEM((8 * DEPTH, COLS), jnp.bfloat16),
            pltpu.VMEM((COLS, 8 * DEPTH), jnp.bfloat16),
            pltpu.VMEM((8, DEPTH // 128, 128), jnp.float32),
            dma((2,)),
            dma((2, N)), dma((2, N)), dma((2, N)), dma((2, N)),
            dma((4,)), dma((4,)),
            dma((2, N)), dma((2, N)), dma((2, N)), dma((2, N)),
            dma((2, CHUNKS)), dma((2, CHUNKS)),
            dma((7,)), dma((7,)),
        ],
        compiler_params=pltpu.CompilerParams(collective_id=0, has_side_effects=True),
        cost_estimate=pl.CostEstimate(flops=2 * 8 * DEPTH * ROWS * COLS, bytes_accessed=4 << 20, transcendentals=0),
    )(slab, weight)


def on_device(pair_slab, pair_weights):
    return gather_and_multiply(pair_slab, pair_weights.reshape(DEPTH // 128, 128)).T


def solution(mesh):
    placed = (P("pair", "row"), P("pair"))
    return jax.shard_map(
        on_device, mesh=mesh, in_specs=placed, out_specs=P("row", ("col", "pair")), check_vma=False
    )
```

```python
import functools
import jax
import jax.numpy as jnp
from jax import lax
from jax.experimental import pallas as pl
from jax.experimental.pallas import tpu as pltpu
from jax.sharding import PartitionSpec as P

MESH = pl.DeviceIdType.MESH
NX, NY, NZ, NYL = 4, 8, 8, 4
DEPTH, ROWS, COLS = 384, 2048, 256
QUARTER, UNIT = ROWS // 4, DEPTH // 4

SLOTS = (
    (0, 1, 1), (0, 2, 1), (0, 1, 0), (1, 1, 1), (0, 3, 1), (0, 2, 0),
    (0, 0, 1), (1, 2, 1), (0, 3, 0), (1, 3, 1), (0, 0, 0), (1, 0, 1),
)
N = len(SLOTS)
FLIGHT = 5
XL = SL = 4

UNITS, ONE_WAY = 11, 5
CHUNKS = 2 * UNITS
BLOCK = sum(v << (2 * n) for n, v in enumerate((0, 0, 1, 3, 1, 2, 2, 3, 3, 2, 2)))
PART = sum(v << (2 * n) for n, v in enumerate((0, 1, 2, 2, 3, 2, 2, 3, 3, 3, 3)))
OTHER = sum(v << (2 * n) for n, v in enumerate((0, 0, 0, 0, 0, 0, 1, 0, 1, 0, 1)))
REACH = (4, 3)
NEEDS = {0: (0, 1), 1: (2, 3, 4, 7, 8), 2: (5, 6, 9, 10)}
HOP = 3
LAST = 20 + HOP * 4
PRODUCTS = {
    22: ((0, 0),), 23: ((0, 2),), 24: ((0, 1),), 25: ((0, 3),),
    29: ((-1, 0), (1, 0), (-1, 1), (1, 3)), 30: ((-1, 2), (1, 2)), 31: ((-1, 3), (1, 1)),
    LAST: ((2, 0), (2, 2), (2, 1), (2, 3)),
}
SCALES = {22: (0,), 29: (-1, 1), LAST: (2,)}


def schedule():
    after, last = {}, -1
    for s in range(2 * N):
        kind, q, low = SLOTS[s // 2]
        need = s - FLIGHT
        if kind:
            need = max(need, 2 * SLOTS.index((0, (q + 1) % 4, low)) + s % 2)
        last = max(last, need)
        after.setdefault(last, []).append(s)
    return after


def mod(value, n):
    return lax.rem(value + 4 * n, n)


def kernel(slab, weight, out, panel, ring, other, scaled, wbuf, local, ysend, yrecv, xsend, xrecv, osend, orecv,
           sysend, syrecv, sxsend, sxrecv, zsend, zrecv, hsend, hrecv, wsend, wrecv):
    z, col, pair = lax.axis_index("row"), lax.axis_index("col"), lax.axis_index("pair")
    x, yh, yl, c = col // 2, lax.rem(col, 2), pair // 2, lax.rem(pair, 2)
    y = yh * NYL + yl
    half = lax.rem(x, 2)

    def device(xx, yy, zz, cc):
        xx, yy, zz = mod(xx, NX), mod(yy, NY), mod(zz, NZ)
        return (zz, xx * 2 + yy // NYL, lax.rem(yy, NYL) * 2 + cc)

    ys = (device(x, y + 1, z, c), device(x, y - 1, z, c))
    xs = (device(x + 1, y, z, c), device(x - 1, y, z, c))
    zs = (device(x, y, z + 1, c), device(x, y, z - 1, c))
    sibling = device(x, y, z, 1 - c)

    def block(rel, flip):
        core = c + flip - 2 * c * flip
        return mod(yl + rel, NYL) * 2 + core

    def rows_at(rel, flip, group):
        return pl.ds(pl.multiple_of(block(rel, flip) * DEPTH + group * UNIT, 32), UNIT)

    def quarter_at(rel):
        return pl.ds(pl.multiple_of(mod(yl + rel, 4) * QUARTER, QUARTER), QUARTER)

    def unit(rel, flip, q, group, h=None):
        if h is None:
            return panel.at[rows_at(rel, flip, group), quarter_at(q)]
        first = block(rel, flip) * DEPTH + group * UNIT + h * (UNIT // 2)
        return panel.at[pl.ds(pl.multiple_of(first, 16), UNIT // 2), quarter_at(q)]

    def remote(src, dst, send, recv, to):
        return pltpu.make_async_remote_copy(
            src_ref=src, dst_ref=dst, send_sem=send, recv_sem=recv, device_id=to, device_id_type=MESH
        )

    def group_of(d, low, own_half=True):
        return 2 * (half if own_half else 1 - half) + (low if d == 0 else 1 - low)

    def y_out(d, u):
        sign = 1 - 2 * d
        kind, q, low = SLOTS[u // 2]
        piece = unit(-sign * kind, 0, sign * q, group_of(d, low), u % 2)
        return remote(piece, piece, ysend.at[d, u], yrecv.at[d, u], ys[d])

    def arrived(d, t, own_half=True, flip=0, h=None):
        sign = 1 - 2 * d
        kind, q, low = SLOTS[t]
        return unit(-sign * (1 + kind), flip, sign * (q - 1), group_of(d, low, own_half), h)

    def y_in(d, u):
        piece = arrived(d, u // 2, h=u % 2)
        return remote(piece, piece, ysend.at[d, u], yrecv.at[d, u], ys[1 - d])

    def side(e, t):
        low = SLOTS[t][2]
        return 0 if low == e else 1

    def x_out(e, u):
        piece = arrived(side(e, u // 2), u // 2, h=u % 2)
        return remote(piece, piece, xsend.at[e, u], xrecv.at[e, u], xs[e])

    def x_in(e, u):
        piece = arrived(side(e, u // 2), u // 2, own_half=False, h=u % 2)
        return remote(piece, piece, xsend.at[e, u], xrecv.at[e, u], xs[1 - e])

    def sy(d, t, flip):
        piece = arrived(d, t, flip=flip)
        return remote(piece, piece, sysend.at[d, t], syrecv.at[d, t], sibling)

    def sx(e, t, flip):
        piece = arrived(side(e, t), t, own_half=False, flip=flip)
        return remote(piece, piece, sxsend.at[e, t], sxrecv.at[e, t], sibling)

    def own(q, flip):
        piece = panel.at[pl.ds(pl.multiple_of(block(0, flip) * DEPTH, DEPTH), DEPTH), quarter_at(q)]
        return remote(piece, piece, osend.at[q], orecv.at[q], sibling)

    def weights(n, rel, flip, to):
        piece = wbuf.at[block(rel, flip)]
        return remote(piece, piece, wsend.at[n], wrecv.at[n], to)

    column = pl.ds(pl.multiple_of(pair * COLS, COLS), COLS)
    distance = (mod(z - col, NZ), mod(col - z, NZ))

    wide = quarter_at(0)
    left = pl.ds(pl.multiple_of(c * COLS, COLS), COLS)
    right = pl.ds(pl.multiple_of((1 - c) * COLS, COLS), COLS)

    def ring_rows(d, n, h=None):
        swap = (OTHER >> (2 * n)) & 1
        group = swap if d == 0 else 1 - swap
        rel = mod(yl + (1 - 2 * group) * ((BLOCK >> (2 * n)) & 3), NYL)
        code = (PART >> (2 * n)) & 3
        by_half = code // 2
        part = by_half * lax.rem(half + code, 2) + (1 - by_half) * code
        inside = (2 * part + group) * UNIT
        if h is None:
            return pl.ds(pl.multiple_of(rel * DEPTH + inside, 32), UNIT)
        inside = inside + h * (UNIT // 2)
        return tuple(pl.ds(pl.multiple_of(first * DEPTH + inside, 16), UNIT // 2) for first in (rel, 2 * rel + c))

    def hand_over(d, n):
        rows = ring_rows(d, n)
        return remote(ring.at[rows, right], other.at[rows], hsend.at[d, n], hrecv.at[d, n], sibling)

    def hand_in(d, n):
        rows = ring_rows(d, n)
        return remote(other.at[rows], other.at[rows], hsend.at[d, n], hrecv.at[d, n], sibling)

    def reaches(d, n):
        reach = NZ - 1 if n < ONE_WAY else REACH[d]
        return (distance[d] > 0) & (distance[d] <= reach), distance[d] < reach

    def z_step(u):
        for d in range(2):
            w = u - HOP * distance[d]
            late = (w + 64) // 69
            k = w + 2 - late

            @pl.when((w >= -2) & (w != 4) & (k < CHUNKS))
            def _(d=d, k=k):
                n, h = k // 2, lax.rem(k, 2)
                rows, source_rows = ring_rows(d, n, h)
                reach = NZ - 1 - (NZ - 1 - REACH[d]) * jnp.minimum(k // (2 * ONE_WAY), 1)
                sems = zsend.at[d, k], zrecv.at[d, k]

                @pl.when(distance[d] == 0)
                def _():
                    remote(panel.at[source_rows, wide], ring.at[rows], *sems, zs[d]).start()

                @pl.when((distance[d] > 0) & (distance[d] <= reach))
                def _():
                    remote(ring.at[rows], ring.at[rows], *sems, zs[1 - d]).wait_recv()

                    @pl.when(distance[d] < reach)
                    def _():
                        remote(ring.at[rows], ring.at[rows], *sems, zs[d]).start()

                    @pl.when(h == 1)
                    def _():
                        hand_over(d, n).start()

    def scale(rel):
        for n in NEEDS[abs(rel)]:
            for d in range(2):
                if rel == -1:

                    @pl.when(reaches(d, n)[0])
                    def _(d=d, n=n):
                        hand_in(d, n).wait_recv()

                elif rel != 1:

                    @pl.when(reaches(d, n)[0])
                    def _(d=d, n=n):
                        hand_in(d, n).wait_recv()

        first = mod(yl + rel, NYL)
        for flip in range(2):
            b = block(rel, flip)
            for i in range(DEPTH // 128):
                at = pl.multiple_of(b * DEPTH + i * 128, 128)
                rows = pl.ds(pl.multiple_of(first * DEPTH + i * 128, 128), 128)
                w = wbuf[b, pl.ds(i, 1), :]

                @pl.when(z == col)
                def _(at=at, w=w):
                    tile = panel[pl.ds(at, 128), column].astype(jnp.float32)
                    scaled[:, pl.ds(at, 128)] = (jnp.transpose(tile) * w).astype(jnp.bfloat16)

                @pl.when(z != col)
                def _(at=at, w=w, rows=rows, flip=flip):
                    tile = (other[rows, :] if flip else ring[rows, left]).astype(jnp.float32)
                    scaled[:, pl.ds(at, 128)] = (jnp.transpose(tile) * w).astype(jnp.bfloat16)

    def multiply(rel, q):
        at = pl.ds(pl.multiple_of(mod(yl + rel, NYL) * 2 * DEPTH, 2 * DEPTH), 2 * DEPTH)
        where = quarter_at(q)
        value = jnp.dot(scaled[:, at], panel[at, where], preferred_element_type=jnp.float32)
        if rel == 0:
            out[:, where] = value
        else:
            out[:, where] += value

    mine = pltpu.make_async_copy(slab, panel.at[pl.ds(pl.multiple_of(pair * DEPTH, DEPTH), DEPTH)], local.at[0])
    mine.start()
    my_weights = pltpu.make_async_copy(weight, wbuf.at[pair], local.at[1])
    my_weights.start()
    barrier = pltpu.get_barrier_semaphore()
    partners = ys + xs + zs + (sibling,)
    for to in partners:
        pl.semaphore_signal(barrier, inc=1, device_id=to, device_id_type=MESH)
    mine.wait()
    my_weights.wait()
    pl.semaphore_wait(barrier, len(partners))

    after = schedule()
    for s in after[-1]:
        for d in range(2):
            y_out(d, s).start()
    own(0, 0).start()
    z_step(-2)
    z_step(-1)
    for q in range(1, 4):
        own(q, 0).start()
    weights(0, 0, 0, ys[0]).start()
    weights(1, 0, 0, ys[1]).start()
    weights(2, 0, 0, sibling).start()

    for u in range(LAST + 1):
        if u < 2 * N:
            for d in range(2):
                y_in(d, u).wait_recv()
            for s in after.get(u, ()):
                for d in range(2):
                    y_out(d, s).start()
            for e in range(2):
                x_out(e, u).start()
            if u % 2:
                for d in range(2):
                    sy(d, u // 2, 0).start()
        if u == 0:
            own(0, 1).wait_recv()
        if u % 2 and 0 <= u - 1 - SL < 2 * N:
            for d in range(2):
                sy(d, (u - 1 - SL) // 2, 1).wait_recv()
        if 0 <= u - XL < 2 * N:
            for e in range(2):
                x_in(e, u - XL).wait_recv()
            if u % 2:
                for e in range(2):
                    sx(e, (u - 1 - XL) // 2, 0).start()
        if u % 2 and 0 <= u - 1 - XL - SL < 2 * N:
            for e in range(2):
                sx(e, (u - 1 - XL - SL) // 2, 1).wait_recv()
        z_step(u)
        if u == 2:
            weights(0, -1, 0, ys[1]).wait_recv()
            weights(1, 1, 0, ys[0]).wait_recv()
            weights(2, 0, 1, sibling).wait_recv()
            weights(3, -1, 0, ys[0]).start()
            weights(4, -1, 0, sibling).start()
            weights(5, 1, 0, sibling).start()
        if u == 4:
            for q in range(1, 4):
                own(q, 1).wait_recv()
        if u == 8:
            weights(3, 2, 0, ys[1]).wait_recv()
            weights(6, 2, 0, sibling).start()
            weights(4, -1, 1, sibling).wait_recv()
            weights(5, 1, 1, sibling).wait_recv()
        if u == 12:
            weights(6, 2, 1, sibling).wait_recv()
        for rel in SCALES.get(u, ()):
            scale(rel)
        for rel, q in PRODUCTS.get(u, ()):
            multiply(rel, q)

    for u in range(2 * N):
        for d in range(2):
            y_out(d, u).wait_send()
            x_out(d, u).wait_send()
    for t in range(N):
        for d in range(2):
            sy(d, t, 0).wait_send()
            sx(d, t, 0).wait_send()
    for q in range(4):
        own(q, 0).wait_send()
    for n, (rel, to) in enumerate(((0, ys[0]), (0, ys[1]), (0, sibling), (-1, ys[0]), (-1, sibling), (1, sibling), (2, sibling))):
        weights(n, rel, 0, to).wait_send()
    for d in range(2):
        for low, high in ((0, ONE_WAY), (ONE_WAY, UNITS)):

            @pl.when(reaches(d, low)[1])
            def _(d=d, low=low, high=high):
                for k in range(2 * low, 2 * high):
                    rows = pl.ds(0, UNIT // 2)
                    remote(ring.at[rows], ring.at[rows], zsend.at[d, k], zrecv.at[d, k], zs[d]).wait_send()

            @pl.when(reaches(d, low)[0])
            def _(d=d, low=low, high=high):
                for n in range(low, high):
                    hand_over(d, n).wait_send()


def gather_and_multiply(slab, weight):
    dma = pltpu.SemaphoreType.DMA
    return pl.pallas_call(
        kernel,
        out_shape=jax.ShapeDtypeStruct((COLS, ROWS), jnp.float32),
        in_specs=[pl.BlockSpec(memory_space=pltpu.HBM)] * 2,
        out_specs=pl.BlockSpec(memory_space=pltpu.VMEM),
        scratch_shapes=[
            pltpu.VMEM((8 * DEPTH, ROWS), jnp.bfloat16),
            pltpu.VMEM((4 * DEPTH, 2 * COLS), jnp.bfloat16),
            pltpu.VMEM((4 * DEPTH, COLS), jnp.bfloat16),
            pltpu.VMEM((COLS, 8 * DEPTH), jnp.bfloat16),
            pltpu.VMEM((8, DEPTH // 128, 128), jnp.float32),
            dma((2,)),
            dma((2, 2 * N)), dma((2, 2 * N)), dma((2, 2 * N)), dma((2, 2 * N)),
            dma((4,)), dma((4,)),
            dma((2, N)), dma((2, N)), dma((2, N)), dma((2, N)),
            dma((2, CHUNKS)), dma((2, CHUNKS)),
            dma((2, UNITS)), dma((2, UNITS)),
            dma((7,)), dma((7,)),
        ],
        compiler_params=pltpu.CompilerParams(collective_id=0, has_side_effects=True, vmem_limit_bytes=30 << 20),
        cost_estimate=pl.CostEstimate(flops=2 * 8 * DEPTH * ROWS * COLS, bytes_accessed=4 << 20, transcendentals=0),
    )(slab, weight)


def on_device(pair_slab, pair_weights):
    return gather_and_multiply(pair_slab, pair_weights.reshape(DEPTH // 128, 128)).T


def solution(mesh):
    placed = (P("pair", "row"), P("pair"))
    return jax.shard_map(
        on_device, mesh=mesh, in_specs=placed, out_specs=P("row", ("col", "pair")), check_vma=False
    )
```

```python
import functools
import jax
import jax.numpy as jnp
from jax import lax
from jax.experimental import pallas as pl
from jax.experimental.pallas import tpu as pltpu
from jax.sharding import PartitionSpec as P

MESH = pl.DeviceIdType.MESH
NX, NY, NZ, NYL = 4, 8, 8, 4
DEPTH, ROWS, COLS = 384, 2048, 256
QUARTER, UNIT = ROWS // 4, DEPTH // 4

SLOTS = (
    (0, 1, 1), (0, 2, 1), (0, 1, 0), (1, 1, 1), (0, 3, 1), (0, 2, 0),
    (0, 0, 1), (1, 2, 1), (0, 3, 0), (1, 3, 1), (0, 0, 0), (1, 0, 1),
)
N = len(SLOTS)
FLIGHT = 5
XL = SL = 4

UNITS, ONE_WAY = 11, 5
CHUNKS = 2 * UNITS
BLOCK = sum(v << (2 * n) for n, v in enumerate((0, 0, 1, 3, 1, 2, 2, 3, 3, 2, 2)))
PART = sum(v << (2 * n) for n, v in enumerate((0, 1, 2, 2, 3, 2, 2, 3, 3, 3, 3)))
OTHER = sum(v << (2 * n) for n, v in enumerate((0, 0, 0, 0, 0, 0, 1, 0, 1, 0, 1)))
REACH = (4, 3)
NEEDS = {0: (0, 1), 1: (2, 3, 4, 7, 8), 2: (5, 6, 9, 10)}
HOP = 3
LAST = 20 + HOP * 4
PRODUCTS = {
    22: ((0, 0),), 23: ((0, 2),), 24: ((0, 1),), 25: ((0, 3),),
    29: ((-1, 0), (1, 0), (-1, 1), (1, 3)), 30: ((-1, 2), (1, 2)), 31: ((-1, 3), (1, 1)),
    LAST: ((2, 0), (2, 2), (2, 1), (2, 3)),
}
SCALES = {22: (0,), 29: (-1, 1), LAST: (2,)}


def schedule():
    after, last = {}, -1
    for s in range(2 * N):
        kind, q, low = SLOTS[s // 2]
        need = s - FLIGHT
        if kind:
            need = max(need, 2 * SLOTS.index((0, (q + 1) % 4, low)) + s % 2)
        last = max(last, need)
        after.setdefault(last, []).append(s)
    return after


def mod(value, n):
    return lax.rem(value + 4 * n, n)


def kernel(slab, weight, out, panel, ring, other, scaled, wbuf, local, ysend, yrecv, xsend, xrecv, osend, orecv,
           sysend, syrecv, sxsend, sxrecv, zsend, zrecv, hsend, hrecv, wsend, wrecv):
    z, col, pair = lax.axis_index("row"), lax.axis_index("col"), lax.axis_index("pair")
    x, yh, yl, c = col // 2, lax.rem(col, 2), pair // 2, lax.rem(pair, 2)
    y = yh * NYL + yl
    half = lax.rem(x, 2)

    def device(xx, yy, zz, cc):
        xx, yy, zz = mod(xx, NX), mod(yy, NY), mod(zz, NZ)
        return (zz, xx * 2 + yy // NYL, lax.rem(yy, NYL) * 2 + cc)

    ys = (device(x, y + 1, z, c), device(x, y - 1, z, c))
    xs = (device(x + 1, y, z, c), device(x - 1, y, z, c))
    zs = (device(x, y, z + 1, c), device(x, y, z - 1, c))
    sibling = device(x, y, z, 1 - c)

    def block(rel, flip):
        core = c + flip - 2 * c * flip
        return mod(yl + rel, NYL) * 2 + core

    def rows_at(rel, flip, group):
        return pl.ds(pl.multiple_of(block(rel, flip) * DEPTH + group * UNIT, 32), UNIT)

    def quarter_at(rel):
        return pl.ds(pl.multiple_of(mod(yl + rel, 4) * QUARTER, QUARTER), QUARTER)

    def unit(rel, flip, q, group, h=None):
        if h is None:
            return panel.at[rows_at(rel, flip, group), quarter_at(q)]
        first = block(rel, flip) * DEPTH + group * UNIT + h * (UNIT // 2)
        return panel.at[pl.ds(pl.multiple_of(first, 16), UNIT // 2), quarter_at(q)]

    def remote(src, dst, send, recv, to):
        return pltpu.make_async_remote_copy(
            src_ref=src, dst_ref=dst, send_sem=send, recv_sem=recv, device_id=to, device_id_type=MESH
        )

    def group_of(d, low, own_half=True):
        return 2 * (half if own_half else 1 - half) + (low if d == 0 else 1 - low)

    def y_out(d, u):
        sign = 1 - 2 * d
        kind, q, low = SLOTS[u // 2]
        piece = unit(-sign * kind, 0, sign * q, group_of(d, low), u % 2)
        return remote(piece, piece, ysend.at[d, u], yrecv.at[d, u], ys[d])

    def arrived(d, t, own_half=True, flip=0, h=None):
        sign = 1 - 2 * d
        kind, q, low = SLOTS[t]
        return unit(-sign * (1 + kind), flip, sign * (q - 1), group_of(d, low, own_half), h)

    def y_in(d, u):
        piece = arrived(d, u // 2, h=u % 2)
        return remote(piece, piece, ysend.at[d, u], yrecv.at[d, u], ys[1 - d])

    def side(e, t):
        low = SLOTS[t][2]
        return 0 if low == e else 1

    def x_out(e, u):
        piece = arrived(side(e, u // 2), u // 2, h=u % 2)
        return remote(piece, piece, xsend.at[e, u], xrecv.at[e, u], xs[e])

    def x_in(e, u):
        piece = arrived(side(e, u // 2), u // 2, own_half=False, h=u % 2)
        return remote(piece, piece, xsend.at[e, u], xrecv.at[e, u], xs[1 - e])

    def sy(d, t, flip):
        piece = arrived(d, t, flip=flip)
        return remote(piece, piece, sysend.at[d, t], syrecv.at[d, t], sibling)

    def sx(e, t, flip):
        piece = arrived(side(e, t), t, own_half=False, flip=flip)
        return remote(piece, piece, sxsend.at[e, t], sxrecv.at[e, t], sibling)

    def own(q, flip):
        piece = panel.at[pl.ds(pl.multiple_of(block(0, flip) * DEPTH, DEPTH), DEPTH), quarter_at(q)]
        return remote(piece, piece, osend.at[q], orecv.at[q], sibling)

    def weights(n, rel, flip, to):
        piece = wbuf.at[block(rel, flip)]
        return remote(piece, piece, wsend.at[n], wrecv.at[n], to)

    column = pl.ds(pl.multiple_of(pair * COLS, COLS), COLS)
    distance = (mod(z - col, NZ), mod(col - z, NZ))

    wide = quarter_at(0)
    left = pl.ds(pl.multiple_of(c * COLS, COLS), COLS)
    right = pl.ds(pl.multiple_of((1 - c) * COLS, COLS), COLS)

    def ring_rows(d, n, h=None):
        swap = (OTHER >> (2 * n)) & 1
        group = swap if d == 0 else 1 - swap
        rel = mod(yl + (1 - 2 * group) * ((BLOCK >> (2 * n)) & 3), NYL)
        code = (PART >> (2 * n)) & 3
        by_half = code // 2
        part = by_half * lax.rem(half + code, 2) + (1 - by_half) * code
        inside = (2 * part + group) * UNIT
        if h is None:
            return pl.ds(pl.multiple_of(rel * DEPTH + inside, 32), UNIT)
        inside = inside + h * (UNIT // 2)
        return tuple(pl.ds(pl.multiple_of(first * DEPTH + inside, 16), UNIT // 2) for first in (rel, 2 * rel + c))

    def hand_over(d, n):
        rows = ring_rows(d, n)
        return remote(ring.at[rows, right], other.at[rows], hsend.at[d, n], hrecv.at[d, n], sibling)

    def hand_in(d, n):
        rows = ring_rows(d, n)
        return remote(other.at[rows], other.at[rows], hsend.at[d, n], hrecv.at[d, n], sibling)

    def reaches(d, n):
        reach = NZ - 1 if n < ONE_WAY else REACH[d]
        return (distance[d] > 0) & (distance[d] <= reach), distance[d] < reach

    def z_step(u):
        for d in range(2):
            w = u - HOP * distance[d]
            late = (w + 64) // 69
            k = w + 2 - late

            @pl.when((w >= -2) & (w != 4) & (k < CHUNKS))
            def _(d=d, k=k):
                n, h = k // 2, lax.rem(k, 2)
                rows, source_rows = ring_rows(d, n, h)
                reach = NZ - 1 - (NZ - 1 - REACH[d]) * jnp.minimum(k // (2 * ONE_WAY), 1)
                sems = zsend.at[d, k], zrecv.at[d, k]

                @pl.when(distance[d] == 0)
                def _():
                    remote(panel.at[source_rows, wide], ring.at[rows], *sems, zs[d]).start()

                @pl.when((distance[d] > 0) & (distance[d] <= reach))
                def _():
                    remote(ring.at[rows], ring.at[rows], *sems, zs[1 - d]).wait_recv()

                    @pl.when(distance[d] < reach)
                    def _():
                        remote(ring.at[rows], ring.at[rows], *sems, zs[d]).start()

                    @pl.when(h == 1)
                    def _():
                        hand_over(d, n).start()

    def scale(rel):
        for n in NEEDS[abs(rel)]:
            for d in range(2):
                if rel == -1:

                    @pl.when(reaches(d, n)[0])
                    def _(d=d, n=n):
                        hand_in(d, n).wait_recv()

                elif rel != 1:

                    @pl.when(reaches(d, n)[0])
                    def _(d=d, n=n):
                        hand_in(d, n).wait_recv()

        first = mod(yl + rel, NYL)
        for flip in range(2):
            b = block(rel, flip)
            for i in range(DEPTH // 128):
                at = pl.multiple_of(b * DEPTH + i * 128, 128)
                rows = pl.ds(pl.multiple_of(first * DEPTH + i * 128, 128), 128)
                w = wbuf[b, pl.ds(i, 1), :]

                @pl.when(z == col)
                def _(at=at, w=w):
                    tile = panel[pl.ds(at, 128), column].astype(jnp.float32)
                    scaled[:, pl.ds(at, 128)] = (jnp.transpose(tile) * w).astype(jnp.bfloat16)

                @pl.when(z != col)
                def _(at=at, w=w, rows=rows, flip=flip):
                    tile = (other[rows, :] if flip else ring[rows, left]).astype(jnp.float32)
                    scaled[:, pl.ds(at, 128)] = (jnp.transpose(tile) * w).astype(jnp.bfloat16)

    def multiply(rel, q):
        at = pl.ds(pl.multiple_of(mod(yl + rel, NYL) * 2 * DEPTH, 2 * DEPTH), 2 * DEPTH)
        where = quarter_at(q)
        value = jnp.dot(scaled[:, at], panel[at, where], preferred_element_type=jnp.float32)
        if rel == 0:
            out[:, where] = value
        else:
            out[:, where] += value

    mine = pltpu.make_async_copy(slab, panel.at[pl.ds(pl.multiple_of(pair * DEPTH, DEPTH), DEPTH)], local.at[0])
    mine.start()
    my_weights = pltpu.make_async_copy(weight, wbuf.at[pair], local.at[1])
    my_weights.start()
    barrier = pltpu.get_barrier_semaphore()
    partners = ys + xs + zs + (sibling,)
    for to in partners:
        pl.semaphore_signal(barrier, inc=1, device_id=to, device_id_type=MESH)
    mine.wait()
    my_weights.wait()
    pl.semaphore_wait(barrier, len(partners))

    after = schedule()
    for s in after[-1]:
        for d in range(2):
            y_out(d, s).start()
    own(0, 0).start()
    z_step(-2)
    z_step(-1)
    for q in range(1, 4):
        own(q, 0).start()
    weights(0, 0, 0, ys[0]).start()
    weights(1, 0, 0, ys[1]).start()
    weights(2, 0, 0, sibling).start()

    for u in range(LAST + 1):
        if u < 2 * N:
            for d in range(2):
                y_in(d, u).wait_recv()
            for s in after.get(u, ()):
                for d in range(2):
                    y_out(d, s).start()
            for e in range(2):
                x_out(e, u).start()
            if u % 2:
                for d in range(2):
                    sy(d, u // 2, 0).start()
        if u == 0:
            own(0, 1).wait_recv()
        if u % 2 and 0 <= u - 1 - SL < 2 * N:
            for d in range(2):
                sy(d, (u - 1 - SL) // 2, 1).wait_recv()
        if 0 <= u - XL < 2 * N:
            for e in range(2):
                x_in(e, u - XL).wait_recv()
            if u % 2:
                for e in range(2):
                    sx(e, (u - 1 - XL) // 2, 0).start()
        if u % 2 and 0 <= u - 1 - XL - SL < 2 * N:
            for e in range(2):
                sx(e, (u - 1 - XL - SL) // 2, 1).wait_recv()
        z_step(u)
        if u == 2:
            weights(0, -1, 0, ys[1]).wait_recv()
            weights(1, 1, 0, ys[0]).wait_recv()
            weights(2, 0, 1, sibling).wait_recv()
            weights(3, -1, 0, ys[0]).start()
            weights(4, -1, 0, sibling).start()
            weights(5, 1, 0, sibling).start()
        if u == 4:
            for q in range(1, 4):
                own(q, 1).wait_recv()
        if u == 8:
            weights(3, 2, 0, ys[1]).wait_recv()
            weights(6, 2, 0, sibling).start()
            weights(4, -1, 1, sibling).wait_recv()
            weights(5, 1, 1, sibling).wait_recv()
        if u == 12:
            weights(6, 2, 1, sibling).wait_recv()
        for rel in SCALES.get(u, ()):
            scale(rel)
        for rel, q in PRODUCTS.get(u, ()):
            multiply(rel, q)

    for u in range(2 * N):
        for d in range(2):
            y_out(d, u).wait_send()
            x_out(d, u).wait_send()
    for t in range(N):
        for d in range(2):
            sy(d, t, 0).wait_send()
            sx(d, t, 0).wait_send()
    for q in range(4):
        own(q, 0).wait_send()
    for n, (rel, to) in enumerate(((0, ys[0]), (0, ys[1]), (0, sibling), (-1, ys[0]), (-1, sibling), (1, sibling), (2, sibling))):
        weights(n, rel, 0, to).wait_send()
    for d in range(2):
        for low, high in ((0, ONE_WAY), (ONE_WAY, UNITS)):

            @pl.when(reaches(d, low)[1])
            def _(d=d, low=low, high=high):
                for k in range(2 * low, 2 * high):
                    rows = pl.ds(0, UNIT // 2)
                    remote(ring.at[rows], ring.at[rows], zsend.at[d, k], zrecv.at[d, k], zs[d]).wait_send()

            @pl.when(reaches(d, low)[0])
            def _(d=d, low=low, high=high):
                for n in range(low, high):
                    hand_over(d, n).wait_send()


def gather_and_multiply(slab, weight):
    dma = pltpu.SemaphoreType.DMA
    return pl.pallas_call(
        kernel,
        out_shape=jax.ShapeDtypeStruct((COLS, ROWS), jnp.float32),
        in_specs=[pl.BlockSpec(memory_space=pltpu.HBM)] * 2,
        out_specs=pl.BlockSpec(memory_space=pltpu.VMEM),
        scratch_shapes=[
            pltpu.VMEM((8 * DEPTH, ROWS), jnp.bfloat16),
            pltpu.VMEM((4 * DEPTH, 2 * COLS), jnp.bfloat16),
            pltpu.VMEM((4 * DEPTH, COLS), jnp.bfloat16),
            pltpu.VMEM((COLS, 8 * DEPTH), jnp.bfloat16),
            pltpu.VMEM((8, DEPTH // 128, 128), jnp.float32),
            dma((2,)),
            dma((2, 2 * N)), dma((2, 2 * N)), dma((2, 2 * N)), dma((2, 2 * N)),
            dma((4,)), dma((4,)),
            dma((2, N)), dma((2, N)), dma((2, N)), dma((2, N)),
            dma((2, CHUNKS)), dma((2, CHUNKS)),
            dma((2, UNITS)), dma((2, UNITS)),
            dma((7,)), dma((7,)),
        ],
        compiler_params=pltpu.CompilerParams(collective_id=0, has_side_effects=True, vmem_limit_bytes=30 << 20),
        cost_estimate=pl.CostEstimate(flops=2 * 8 * DEPTH * ROWS * COLS, bytes_accessed=4 << 20, transcendentals=0),
    )(pltpu.with_memory_space_constraint(slab, pltpu.HBM), pltpu.with_memory_space_constraint(weight, pltpu.HBM))


def on_device(pair_slab, pair_weights):
    return gather_and_multiply(pair_slab, pair_weights.reshape(DEPTH // 128, 128)).T


def solution(mesh):
    placed = (P("pair", "row"), P("pair"))
    return jax.shard_map(
        on_device, mesh=mesh, in_specs=placed, out_specs=P("row", ("col", "pair")), check_vma=False
    )
```

```python
import functools
import jax
import jax.numpy as jnp
from jax import lax
from jax.experimental import pallas as pl
from jax.experimental.pallas import tpu as pltpu
from jax.sharding import PartitionSpec as P

MESH = pl.DeviceIdType.MESH
NX, NY, NZ, NYL = 4, 8, 8, 4
DEPTH, ROWS, COLS = 384, 2048, 256
QUARTER, UNIT = ROWS // 4, DEPTH // 4

SLOTS = (
    (0, 1, 1), (0, 2, 1), (0, 1, 0), (1, 1, 1), (0, 3, 1), (0, 2, 0),
    (0, 0, 1), (1, 2, 1), (0, 3, 0), (1, 3, 1), (0, 0, 0), (1, 0, 1),
)
N = len(SLOTS)
FLIGHT = 5
XL = SL = 4

UNITS, ONE_WAY = 11, 5
CHUNKS = 2 * UNITS
BLOCK = sum(v << (2 * n) for n, v in enumerate((0, 0, 1, 3, 1, 2, 2, 3, 3, 2, 2)))
PART = sum(v << (2 * n) for n, v in enumerate((0, 1, 2, 2, 3, 2, 2, 3, 3, 3, 3)))
OTHER = sum(v << (2 * n) for n, v in enumerate((0, 0, 0, 0, 0, 0, 1, 0, 1, 0, 1)))
REACH = (4, 3)
NEEDS = {0: (0, 1), 1: (2, 3, 4, 7, 8), 2: (5, 6, 9, 10)}
HOP = 3
LAST = 19 + HOP * 4
PRODUCTS = {
    21: ((0, 0),), 22: ((0, 2),), 23: ((0, 1),), 24: ((0, 3),),
    28: ((-1, 0), (1, 0), (-1, 1), (1, 3)), 29: ((-1, 2), (1, 2)), 30: ((-1, 3), (1, 1)),
    LAST: ((2, 0), (2, 2), (2, 1), (2, 3)),
}
SCALES = {21: (0,), 28: (-1, 1), LAST: (2,)}


def schedule():
    after, last = {}, -1
    for s in range(2 * N):
        kind, q, low = SLOTS[s // 2]
        need = s - FLIGHT
        if kind:
            need = max(need, 2 * SLOTS.index((0, (q + 1) % 4, low)) + s % 2)
        last = max(last, need)
        after.setdefault(last, []).append(s)
    return after


def mod(value, n):
    return lax.rem(value + 4 * n, n)


def kernel(slab, weight, out, panel, ring, other, scaled, wbuf, local, ysend, yrecv, xsend, xrecv, osend, orecv,
           sysend, syrecv, sxsend, sxrecv, zsend, zrecv, hsend, hrecv, wsend, wrecv):
    z, col, pair = lax.axis_index("row"), lax.axis_index("col"), lax.axis_index("pair")
    x, yh, yl, c = col // 2, lax.rem(col, 2), pair // 2, lax.rem(pair, 2)
    y = yh * NYL + yl
    half = lax.rem(x, 2)

    def device(xx, yy, zz, cc):
        xx, yy, zz = mod(xx, NX), mod(yy, NY), mod(zz, NZ)
        return (zz, xx * 2 + yy // NYL, lax.rem(yy, NYL) * 2 + cc)

    ys = (device(x, y + 1, z, c), device(x, y - 1, z, c))
    xs = (device(x + 1, y, z, c), device(x - 1, y, z, c))
    zs = (device(x, y, z + 1, c), device(x, y, z - 1, c))
    sibling = device(x, y, z, 1 - c)

    def block(rel, flip):
        core = c + flip - 2 * c * flip
        return mod(yl + rel, NYL) * 2 + core

    def rows_at(rel, flip, group):
        return pl.ds(pl.multiple_of(block(rel, flip) * DEPTH + group * UNIT, 32), UNIT)

    def quarter_at(rel):
        return pl.ds(pl.multiple_of(mod(yl + rel, 4) * QUARTER, QUARTER), QUARTER)

    def unit(rel, flip, q, group, h=None):
        if h is None:
            return panel.at[rows_at(rel, flip, group), quarter_at(q)]
        first = block(rel, flip) * DEPTH + group * UNIT + h * (UNIT // 2)
        return panel.at[pl.ds(pl.multiple_of(first, 16), UNIT // 2), quarter_at(q)]

    def remote(src, dst, send, recv, to):
        return pltpu.make_async_remote_copy(
            src_ref=src, dst_ref=dst, send_sem=send, recv_sem=recv, device_id=to, device_id_type=MESH
        )

    def group_of(d, low, own_half=True):
        return 2 * (half if own_half else 1 - half) + (low if d == 0 else 1 - low)

    def y_out(d, u):
        sign = 1 - 2 * d
        kind, q, low = SLOTS[u // 2]
        piece = unit(-sign * kind, 0, sign * q, group_of(d, low), u % 2)
        return remote(piece, piece, ysend.at[d, u], yrecv.at[d, u], ys[d])

    def arrived(d, t, own_half=True, flip=0, h=None):
        sign = 1 - 2 * d
        kind, q, low = SLOTS[t]
        return unit(-sign * (1 + kind), flip, sign * (q - 1), group_of(d, low, own_half), h)

    def y_in(d, u):
        piece = arrived(d, u // 2, h=u % 2)
        return remote(piece, piece, ysend.at[d, u], yrecv.at[d, u], ys[1 - d])

    def side(e, t):
        low = SLOTS[t][2]
        return 0 if low == e else 1

    def x_out(e, u):
        piece = arrived(side(e, u // 2), u // 2, h=u % 2)
        return remote(piece, piece, xsend.at[e, u], xrecv.at[e, u], xs[e])

    def x_in(e, u):
        piece = arrived(side(e, u // 2), u // 2, own_half=False, h=u % 2)
        return remote(piece, piece, xsend.at[e, u], xrecv.at[e, u], xs[1 - e])

    def sy(d, t, flip):
        piece = arrived(d, t, flip=flip)
        return remote(piece, piece, sysend.at[d, t], syrecv.at[d, t], sibling)

    def sx(e, t, flip):
        piece = arrived(side(e, t), t, own_half=False, flip=flip)
        return remote(piece, piece, sxsend.at[e, t], sxrecv.at[e, t], sibling)

    def own(q, flip):
        piece = panel.at[pl.ds(pl.multiple_of(block(0, flip) * DEPTH, DEPTH), DEPTH), quarter_at(q)]
        return remote(piece, piece, osend.at[q], orecv.at[q], sibling)

    def weights(n, rel, flip, to):
        piece = wbuf.at[block(rel, flip)]
        return remote(piece, piece, wsend.at[n], wrecv.at[n], to)

    column = pl.ds(pl.multiple_of(pair * COLS, COLS), COLS)
    distance = (mod(z - col, NZ), mod(col - z, NZ))

    wide = quarter_at(0)
    left = pl.ds(pl.multiple_of(c * COLS, COLS), COLS)
    right = pl.ds(pl.multiple_of((1 - c) * COLS, COLS), COLS)

    def ring_rows(d, n, h=None):
        swap = (OTHER >> (2 * n)) & 1
        group = swap if d == 0 else 1 - swap
        rel = mod(yl + (1 - 2 * group) * ((BLOCK >> (2 * n)) & 3), NYL)
        code = (PART >> (2 * n)) & 3
        by_half = code // 2
        part = by_half * lax.rem(half + code, 2) + (1 - by_half) * code
        inside = (2 * part + group) * UNIT
        if h is None:
            return pl.ds(pl.multiple_of(rel * DEPTH + inside, 32), UNIT)
        inside = inside + h * (UNIT // 2)
        return tuple(pl.ds(pl.multiple_of(first * DEPTH + inside, 16), UNIT // 2) for first in (rel, 2 * rel + c))

    def hand_over(d, n):
        rows = ring_rows(d, n)
        return remote(ring.at[rows, right], other.at[rows], hsend.at[d, n], hrecv.at[d, n], sibling)

    def hand_in(d, n):
        rows = ring_rows(d, n)
        return remote(other.at[rows], other.at[rows], hsend.at[d, n], hrecv.at[d, n], sibling)

    def reaches(d, n):
        reach = NZ - 1 if n < ONE_WAY else REACH[d]
        return (distance[d] > 0) & (distance[d] <= reach), distance[d] < reach

    def z_step(u):
        for d in range(2):
            w = u - HOP * distance[d] + jnp.minimum(distance[d], 1)
            late = (w + 64) // 69
            k = w + 2 - late

            @pl.when((w >= -2) & (w != 4) & (k < CHUNKS))
            def _(d=d, k=k):
                n, h = k // 2, lax.rem(k, 2)
                rows, source_rows = ring_rows(d, n, h)
                reach = NZ - 1 - (NZ - 1 - REACH[d]) * jnp.minimum(k // (2 * ONE_WAY), 1)
                sems = zsend.at[d, k], zrecv.at[d, k]

                @pl.when(distance[d] == 0)
                def _():
                    remote(panel.at[source_rows, wide], ring.at[rows], *sems, zs[d]).start()

                @pl.when((distance[d] > 0) & (distance[d] <= reach))
                def _():
                    remote(ring.at[rows], ring.at[rows], *sems, zs[1 - d]).wait_recv()

                    @pl.when(distance[d] < reach)
                    def _():
                        remote(ring.at[rows], ring.at[rows], *sems, zs[d]).start()

                    @pl.when(h == 1)
                    def _():
                        hand_over(d, n).start()

    def scale(rel):
        for n in NEEDS[abs(rel)]:
            for d in range(2):
                if rel == -1:

                    @pl.when(reaches(d, n)[0])
                    def _(d=d, n=n):
                        hand_in(d, n).wait_recv()

                elif rel != 1:

                    @pl.when(reaches(d, n)[0])
                    def _(d=d, n=n):
                        hand_in(d, n).wait_recv()

        first = mod(yl + rel, NYL)
        for flip in range(2):
            b = block(rel, flip)
            for i in range(DEPTH // 128):
                at = pl.multiple_of(b * DEPTH + i * 128, 128)
                rows = pl.ds(pl.multiple_of(first * DEPTH + i * 128, 128), 128)
                w = wbuf[b, pl.ds(i, 1), :]

                @pl.when(z == col)
                def _(at=at, w=w):
                    tile = panel[pl.ds(at, 128), column].astype(jnp.float32)
                    scaled[:, pl.ds(at, 128)] = (jnp.transpose(tile) * w).astype(jnp.bfloat16)

                @pl.when(z != col)
                def _(at=at, w=w, rows=rows, flip=flip):
                    tile = (other[rows, :] if flip else ring[rows, left]).astype(jnp.float32)
                    scaled[:, pl.ds(at, 128)] = (jnp.transpose(tile) * w).astype(jnp.bfloat16)

    def multiply(rel, q):
        at = pl.ds(pl.multiple_of(mod(yl + rel, NYL) * 2 * DEPTH, 2 * DEPTH), 2 * DEPTH)
        where = quarter_at(q)
        value = jnp.dot(scaled[:, at], panel[at, where], preferred_element_type=jnp.float32)
        if rel == 0:
            out[:, where] = value
        else:
            out[:, where] += value

    mine = pltpu.make_async_copy(slab, panel.at[pl.ds(pl.multiple_of(pair * DEPTH, DEPTH), DEPTH)], local.at[0])
    mine.start()
    my_weights = pltpu.make_async_copy(weight, wbuf.at[pair], local.at[1])
    my_weights.start()
    barrier = pltpu.get_barrier_semaphore()
    partners = ys + xs + zs + (sibling,)
    for to in partners:
        pl.semaphore_signal(barrier, inc=1, device_id=to, device_id_type=MESH)
    mine.wait()
    my_weights.wait()
    pl.semaphore_wait(barrier, len(partners))

    after = schedule()
    for s in after[-1]:
        for d in range(2):
            y_out(d, s).start()
    own(0, 0).start()
    z_step(-2)
    z_step(-1)
    for q in range(1, 4):
        own(q, 0).start()
    weights(0, 0, 0, ys[0]).start()
    weights(1, 0, 0, ys[1]).start()
    weights(2, 0, 0, sibling).start()

    for u in range(LAST + 1):
        if u < 2 * N:
            for d in range(2):
                y_in(d, u).wait_recv()
            for s in after.get(u, ()):
                for d in range(2):
                    y_out(d, s).start()
            for e in range(2):
                x_out(e, u).start()
            if u % 2:
                for d in range(2):
                    sy(d, u // 2, 0).start()
        if u == 0:
            own(0, 1).wait_recv()
        if u % 2 and 0 <= u - 1 - SL < 2 * N:
            for d in range(2):
                sy(d, (u - 1 - SL) // 2, 1).wait_recv()
        if 0 <= u - XL < 2 * N:
            for e in range(2):
                x_in(e, u - XL).wait_recv()
            if u % 2:
                for e in range(2):
                    sx(e, (u - 1 - XL) // 2, 0).start()
        if u % 2 and 0 <= u - 1 - XL - SL < 2 * N:
            for e in range(2):
                sx(e, (u - 1 - XL - SL) // 2, 1).wait_recv()
        z_step(u)
        if u == 2:
            weights(0, -1, 0, ys[1]).wait_recv()
            weights(1, 1, 0, ys[0]).wait_recv()
            weights(2, 0, 1, sibling).wait_recv()
            weights(3, -1, 0, ys[0]).start()
            weights(4, -1, 0, sibling).start()
            weights(5, 1, 0, sibling).start()
        if u == 4:
            for q in range(1, 4):
                own(q, 1).wait_recv()
        if u == 8:
            weights(3, 2, 0, ys[1]).wait_recv()
            weights(6, 2, 0, sibling).start()
            weights(4, -1, 1, sibling).wait_recv()
            weights(5, 1, 1, sibling).wait_recv()
        if u == 12:
            weights(6, 2, 1, sibling).wait_recv()
        for rel in SCALES.get(u, ()):
            scale(rel)
        for rel, q in PRODUCTS.get(u, ()):
            multiply(rel, q)

    for u in range(2 * N):
        for d in range(2):
            y_out(d, u).wait_send()
            x_out(d, u).wait_send()
    for t in range(N):
        for d in range(2):
            sy(d, t, 0).wait_send()
            sx(d, t, 0).wait_send()
    for q in range(4):
        own(q, 0).wait_send()
    for n, (rel, to) in enumerate(((0, ys[0]), (0, ys[1]), (0, sibling), (-1, ys[0]), (-1, sibling), (1, sibling), (2, sibling))):
        weights(n, rel, 0, to).wait_send()
    for d in range(2):
        for low, high in ((0, ONE_WAY), (ONE_WAY, UNITS)):

            @pl.when(reaches(d, low)[1])
            def _(d=d, low=low, high=high):
                for k in range(2 * low, 2 * high):
                    rows = pl.ds(0, UNIT // 2)
                    remote(ring.at[rows], ring.at[rows], zsend.at[d, k], zrecv.at[d, k], zs[d]).wait_send()

            @pl.when(reaches(d, low)[0])
            def _(d=d, low=low, high=high):
                for n in range(low, high):
                    hand_over(d, n).wait_send()


def gather_and_multiply(slab, weight):
    dma = pltpu.SemaphoreType.DMA
    return pl.pallas_call(
        kernel,
        out_shape=jax.ShapeDtypeStruct((COLS, ROWS), jnp.float32),
        in_specs=[pl.BlockSpec(memory_space=pltpu.HBM)] * 2,
        out_specs=pl.BlockSpec(memory_space=pltpu.VMEM),
        scratch_shapes=[
            pltpu.VMEM((8 * DEPTH, ROWS), jnp.bfloat16),
            pltpu.VMEM((4 * DEPTH, 2 * COLS), jnp.bfloat16),
            pltpu.VMEM((4 * DEPTH, COLS), jnp.bfloat16),
            pltpu.VMEM((COLS, 8 * DEPTH), jnp.bfloat16),
            pltpu.VMEM((8, DEPTH // 128, 128), jnp.float32),
            dma((2,)),
            dma((2, 2 * N)), dma((2, 2 * N)), dma((2, 2 * N)), dma((2, 2 * N)),
            dma((4,)), dma((4,)),
            dma((2, N)), dma((2, N)), dma((2, N)), dma((2, N)),
            dma((2, CHUNKS)), dma((2, CHUNKS)),
            dma((2, UNITS)), dma((2, UNITS)),
            dma((7,)), dma((7,)),
        ],
        compiler_params=pltpu.CompilerParams(collective_id=0, has_side_effects=True, vmem_limit_bytes=30 << 20),
        cost_estimate=pl.CostEstimate(flops=2 * 8 * DEPTH * ROWS * COLS, bytes_accessed=4 << 20, transcendentals=0),
    )(pltpu.with_memory_space_constraint(slab, pltpu.HBM), pltpu.with_memory_space_constraint(weight, pltpu.HBM))


def on_device(pair_slab, pair_weights):
    return gather_and_multiply(pair_slab, pair_weights.reshape(DEPTH // 128, 128)).T


def solution(mesh):
    placed = (P("pair", "row"), P("pair"))
    return jax.shard_map(
        on_device, mesh=mesh, in_specs=placed, out_specs=P("row", ("col", "pair")), check_vma=False
    )
```
